128 devices in a mesh: rep: 8 (over y_lo, z), fsdp: 16 (over y_hi, x, core).
Axes of the slice: x: 4, y: 4 (y_hi: 2, y_lo: 2; y = y_hi * 2 + y_lo), z: 4, core: 2. Of those that a mesh axis runs over, the one named last changes fastest.
Arguments:
- query_rows: bfloat16 [49152, 3072], P(('rep', 'fsdp')), may hold values from -48 to 48
- key_rows: bfloat16 [49152, 3072], P(('rep', 'fsdp')), may hold values from -48 to 48
- value_rows: bfloat16 [49152, 3072], P(('rep', 'fsdp')), may hold values from -6 to 6
- out_grad: bfloat16 [49152, 3072], P(('rep', 'fsdp')), may hold values from -6 to 6
- out_weight: bfloat16 [3072, 3072], P('fsdp'), may hold values from -0.109375 to 0.109375
- segment_ids: int32 [49152], P(('rep', 'fsdp')), may hold values from -1 to 4095, as said below
Outputs:
- query_grad: bfloat16 [49152, 3072], P(('rep', 'fsdp'))
- key_grad: bfloat16 [49152, 3072], P(('rep', 'fsdp'))
- value_grad: bfloat16 [49152, 3072], P(('rep', 'fsdp'))
- weight_grad: float32 [3072, 3072], P('fsdp')
The draws below stay inside these ranges and needn't reach their ends.
Inputs may be any that keep to these rules, and one draw needn't show every extreme that they name: `segment_ids`: each aligned block of 384 rows holds whole images in contiguous runs of rows followed by padding rows with id -1; an image id appears in no other block; every image and every block's live part has a multiple of 12 rows, at least 4 such units live a block; in each aligned run of 16 blocks exactly one block has no padding, and every other block has at most 192 live rows.
All inputs are finite; a program needn't handle non-finite values.
Results may differ from the reference program's by a relative error of at most 0.02.
Values may be sent and summed in bfloat16 or wider, within the bound.
A program may use at most 192 MiB of HBM per device.

```python
import math
import jax
import jax.numpy as jnp
from jax import lax

H = 24
E = 128
DW = 3072
ROWS_DEV = 384
HD = 3072
ROWS_ALL = 49152
N_FSDP = 16


def drawn_pair(key):
    base = jax.random.fold_in(key, 7)
    keys_split = jax.random.split(base, 2)
    width = H * E
    shape = (ROWS_ALL, width)
    query_out = jnp.clip(jax.random.normal(keys_split[0], shape, jnp.float32), -4.0, 4.0)
    key_out = jnp.clip(jax.random.normal(keys_split[1], shape, jnp.float32), -4.0, 4.0)
    return (query_out, key_out)


def draw_query_rows(key, part):
    return drawn_pair(key)[0].astype(jnp.bfloat16)


def draw_key_rows(key, part):
    return drawn_pair(key)[1].astype(jnp.bfloat16)


def draw_segment_ids(key, part):
    base = jax.random.fold_in(key, 11)
    keys_split = jax.random.split(base, 3)
    block_count = ROWS_ALL // ROWS_DEV
    unit_rows = ROWS_DEV // 32
    live_rows = unit_rows * jax.random.randint(keys_split[0], (block_count,), 4, 17)
    full_member = jax.random.randint(keys_split[1], (block_count // N_FSDP,), 0, N_FSDP)
    is_full = jnp.arange(block_count) % N_FSDP == jnp.repeat(full_member, N_FSDP)
    live_rows = jnp.where(is_full, ROWS_DEV, live_rows)
    lengths = unit_rows * jax.random.randint(keys_split[2], (block_count, 32), 1, 17)
    bounds = jnp.cumsum(lengths, axis=1)
    positions = jnp.arange(ROWS_DEV)
    local_ids = jnp.sum((bounds[:, None, :] <= positions[None, :, None]).astype(jnp.int32), axis=2)
    ids = jnp.arange(block_count)[:, None] * 32 + (31 - local_ids)
    ids = jnp.where(positions[None, :] < live_rows[:, None], ids, -1)
    return ids.reshape(ROWS_ALL).astype(jnp.int32)


def level_of(key, shape, cuts, smallest, top_value):
    gain, own = 1.0, jax.random.fold_in(key, 6)
    for position, parts in cuts:
        heights = jnp.exp(jax.random.uniform(jax.random.fold_in(own, position), (parts,), jnp.float32, smallest / len(cuts), top_value / len(cuts)))
        gain = gain * jnp.repeat(heights, shape[position] // parts).reshape([-1 if axis == position else 1 for axis in range(len(shape))])
    return gain


def noise(own_key, extent, deviation, limit, cuts=(), held_as=jnp.bfloat16):
    factor_of = level_of(own_key, extent, cuts, -0.22, 0.18) if cuts else 1.0
    result = jax.random.normal(own_key, extent, jnp.float32) * deviation * factor_of
    return jnp.minimum(jnp.maximum(result, -limit), limit).astype(held_as)


def setup_inputs(seed: int = 0) -> dict:
    arg_keys = jax.random.split(jax.random.key(seed), 7)
    return {
        "query_rows": draw_query_rows(jax.random.fold_in(arg_keys[6], 71), 0),
        "key_rows": draw_key_rows(jax.random.fold_in(arg_keys[6], 71), 0),
        "value_rows": noise(arg_keys[2], (ROWS_ALL, HD), 1.0, 6.0, ((0, 128),)),
        "out_grad": noise(arg_keys[3], (ROWS_ALL, DW), 1.0, 6.0, ((0, 128),)),
        "out_weight": noise(arg_keys[4], (HD, DW), (H * E) ** -0.5, 0.109375, ((0, 16),)),
        "segment_ids": draw_segment_ids(jax.random.fold_in(arg_keys[6], 71), 0),
    }


def attention_grads(query_block, key_block, value_block, grad_block, query_segments, key_segments):
    query_count = query_block.shape[0]
    key_count = key_block.shape[0]
    head_count = query_block.shape[1] // E
    inverse_root = 1.0 / math.sqrt(E)
    query_heads = query_block.reshape(query_count, head_count, E).astype(jnp.float32)
    key_heads = key_block.reshape(key_count, head_count, E).astype(jnp.float32)
    value_heads = value_block.reshape(key_count, head_count, E).astype(jnp.float32)
    grad_heads = grad_block.reshape(query_count, head_count, E).astype(jnp.float32)
    logits = jnp.einsum('qhe,khe->hqk', query_heads, key_heads) * inverse_root
    allowed = (query_segments[:, None] == key_segments[None, :]) & (query_segments[:, None] >= 0)
    masked = jnp.where(allowed[None], logits, -1e+30)
    row_max = lax.optimization_barrier(jnp.max(masked, axis=2, keepdims=True))
    raw_weights = jnp.where(allowed[None], jnp.exp(masked - row_max), 0.0)
    totals = lax.optimization_barrier(jnp.sum(raw_weights, axis=2, keepdims=True))
    totals = jnp.where((query_segments >= 0)[None, :, None], totals, 1.0)
    probs = raw_weights / totals
    probs_half = probs.astype(jnp.bfloat16).astype(jnp.float32)
    attended = jnp.einsum('hqk,khe->qhe', probs_half, value_heads).astype(jnp.bfloat16)
    attended_wide = attended.astype(jnp.float32)
    grad_probs = jnp.einsum('qhe,khe->hqk', grad_heads, value_heads)
    row_dot = jnp.einsum('qhe,qhe->hq', grad_heads, attended_wide)
    grad_logits = (probs * (grad_probs - row_dot[:, :, None])).astype(jnp.bfloat16).astype(jnp.float32)
    grad_query = jnp.einsum('hqk,khe->qhe', grad_logits, key_heads) * inverse_root
    grad_key = jnp.einsum('hqk,qhe->khe', grad_logits, query_heads) * inverse_root
    grad_value = jnp.einsum('hqk,qhe->khe', probs_half, grad_heads)
    return (attended.reshape(query_count, -1), grad_query.reshape(query_count, -1), grad_key.reshape(key_count, -1), grad_value.reshape(key_count, -1))

def reference(query_rows, key_rows, value_rows, out_grad, out_weight, segment_ids):
    block_count = ROWS_ALL // ROWS_DEV
    feature_count = query_rows.shape[1]

    def one_block(totals, inputs):
        query_block, key_block, value_block, grad_block, segment_block = inputs
        grad_attended = jnp.dot(grad_block, out_weight.T, preferred_element_type=jnp.float32).astype(jnp.bfloat16)
        attended, grad_query, grad_key, grad_value = attention_grads(query_block, key_block, value_block, grad_attended, segment_block, segment_block)
        term_half = jnp.dot(attended.T, grad_block, preferred_element_type=jnp.float32).astype(jnp.bfloat16)
        term_half = lax.optimization_barrier(term_half)
        totals = totals + term_half.astype(jnp.float32)
        return (totals, (grad_query.astype(jnp.bfloat16), grad_key.astype(jnp.bfloat16), grad_value.astype(jnp.bfloat16)))
    inputs = (query_rows.reshape(block_count, ROWS_DEV, feature_count), key_rows.reshape(block_count, ROWS_DEV, feature_count), value_rows.reshape(block_count, ROWS_DEV, feature_count), out_grad.reshape(block_count, ROWS_DEV, out_grad.shape[1]), segment_ids.reshape(block_count, ROWS_DEV))
    start_totals = jnp.zeros((feature_count, out_grad.shape[1]), jnp.float32)
    totals, grads = lax.scan(one_block, start_totals, inputs)
    query_grad = grads[0].reshape(ROWS_ALL, feature_count)
    key_grad = grads[1].reshape(ROWS_ALL, feature_count)
    value_grad = grads[2].reshape(ROWS_ALL, feature_count)
    weight_grad = totals * (1.0 / math.sqrt(ROWS_ALL))
    return (query_grad, key_grad, value_grad, weight_grad)
```

```python
import math

import jax
import jax.numpy as jnp
from jax import lax
from jax.experimental import pallas as pl
from jax.experimental.pallas import tpu as pltpu
from jax.sharding import PartitionSpec as P

E = 128
HEADS = 3
LOG2E = 1.4426950408889634
F32 = jnp.float32
BF16 = jnp.bfloat16


def dot(a, b, contract_a, contract_b):
    return lax.dot_general(
        a, b, (((contract_a,), (contract_b,)), ((), ())), preferred_element_type=F32
    )


def forward_kernel(q_ref, k_ref, v_ref, column_ref, row_ref, attended_ref, probs_ref):
    column, row = column_ref[...], row_ref[...]
    live = column >= 0
    bias = jnp.where((column == row) & live, 0.0, -1e30)
    for head in range(HEADS):
        at = slice(head * E, (head + 1) * E)
        logits = dot(q_ref[:, at], k_ref[:, at], 1, 1) * (LOG2E / math.sqrt(E)) + bias
        weights = jnp.exp2(logits - jnp.max(logits, axis=1, keepdims=True))
        total = jnp.sum(weights, axis=1, keepdims=True)
        probs = weights * jnp.where(live, 1.0 / total, 0.0)
        probs_ref[head] = probs
        attended_ref[0, :, at] = dot(probs.astype(BF16), v_ref[:, at], 1, 0).astype(BF16)


def attention_forward(query, key, value, segments):
    rows, features = query.shape
    width = HEADS * E
    steps = features // width
    whole = pl.BlockSpec((rows, width), lambda i: (0, i))
    return pl.pallas_call(
        forward_kernel,
        grid=(steps,),
        in_specs=[
            whole,
            whole,
            whole,
            pl.BlockSpec((rows, 1), lambda i: (0, 0)),
            pl.BlockSpec((1, rows), lambda i: (0, 0)),
        ],
        out_specs=[
            pl.BlockSpec((1, rows, width), lambda i: (i, 0, 0)),
            pl.BlockSpec((HEADS, rows, rows), lambda i: (i, 0, 0)),
        ],
        out_shape=[
            jax.ShapeDtypeStruct((steps, rows, width), BF16),
            jax.ShapeDtypeStruct((steps * HEADS, rows, rows), F32),
        ],
        cost_estimate=pl.CostEstimate(
            flops=8 * rows * rows * features,
            bytes_accessed=24 * rows * features,
            transcendentals=rows * rows * features // E,
        ),
        name="attention_forward",
    )(query, key, value, segments[:, None], segments[None, :])


def backward_kernel(
    core_ref, q_ref, k_ref, v_ref, probs_ref, attended_ref, ga_ref, other_ref, dq_ref, dk_ref, dv_ref
):
    scale = 1.0 / math.sqrt(E)
    half = ga_ref.shape[1] - other_ref.shape[1]
    first = core_ref[0] == 0
    for head in range(HEADS):
        at = slice(head * E, (head + 1) * E)
        own, other = ga_ref[0, half:, at], other_ref[0, :, at]
        grad = jnp.concatenate(
            [ga_ref[0, :half, at], jnp.where(first, own, other), jnp.where(first, other, own)], axis=0
        )
        probs = probs_ref[head]
        row_dot = jnp.sum(
            grad.astype(F32) * attended_ref[0, :, at].astype(F32), axis=1, keepdims=True
        )
        grad_logits = (probs * (dot(grad, v_ref[:, at], 1, 1) - row_dot)).astype(BF16)
        dq_ref[:, at] = (dot(grad_logits, k_ref[:, at], 1, 0) * scale).astype(BF16)
        dk_ref[:, at] = (dot(grad_logits, q_ref[:, at], 0, 0) * scale).astype(BF16)
        dv_ref[:, at] = dot(probs.astype(BF16), grad, 0, 0).astype(BF16)


def attention_backward(core, query, key, value, probs, attended, grads, other):
    rows, features = query.shape
    width = HEADS * E
    steps = features // width
    whole = pl.BlockSpec((rows, width), lambda i, c: (0, i))
    step = lambda a: pl.BlockSpec((1,) + a.shape[1:], lambda i, c: (i, 0, 0))
    return pl.pallas_call(
        backward_kernel,
        grid_spec=pltpu.PrefetchScalarGridSpec(
            num_scalar_prefetch=1,
            grid=(steps,),
            in_specs=[
                whole,
                whole,
                whole,
                pl.BlockSpec((HEADS, rows, rows), lambda i, c: (i, 0, 0)),
                step(attended),
                step(grads),
                step(other),
            ],
            out_specs=[whole, whole, whole],
        ),
        out_shape=[jax.ShapeDtypeStruct((rows, features), BF16)] * 3,
        cost_estimate=pl.CostEstimate(
            flops=16 * rows * rows * features,
            bytes_accessed=30 * rows * features,
            transcendentals=0,
        ),
        name="attention_backward",
    )(core, query, key, value, probs, attended, grads, other)


def weight_kernel(count, order_ref, att_ref, extra_ref, *refs):
    pieces, extra_rows, out_ref = refs[:count], refs[count], refs[count + 1]
    total = dot(extra_ref[...], extra_rows[...], 0, 0)
    for place in range(count):
        total += dot(att_ref[order_ref[place]], pieces[place][...], 0, 0)
    out_ref[...] = total


def weight_gradient(order, attended, attended_extra, pieces, extra_rows, tile=512):
    count, rows, width = attended.shape
    features = pieces[0].shape[1]
    return pl.pallas_call(
        lambda *refs: weight_kernel(count, *refs),
        grid_spec=pltpu.PrefetchScalarGridSpec(
            num_scalar_prefetch=1,
            grid=(features // tile,),
            in_specs=[
                pl.BlockSpec(attended.shape, lambda i, o: (0, 0, 0)),
                pl.BlockSpec(attended_extra.shape, lambda i, o: (0, 0)),
            ]
            + [pl.BlockSpec((rows, tile), lambda i, o: (0, i))] * count
            + [pl.BlockSpec((extra_rows.shape[0], tile), lambda i, o: (0, i))],
            out_specs=pl.BlockSpec((width, tile), lambda i, o: (0, i)),
        ),
        out_shape=jax.ShapeDtypeStruct((width, features), F32),
        cost_estimate=pl.CostEstimate(
            flops=2 * width * features * (count * rows + extra_rows.shape[0]),
            bytes_accessed=2 * features * (count * rows + 2 * width),
            transcendentals=0,
        ),
        name="weight_gradient",
    )(order, attended, attended_extra, *pieces, extra_rows)


def moves(across, along, size):
    out = []
    for f in range(2 * 2 * size):
        y, x, c = f // (2 * size), (f // 2) % size, f % 2
        out.append((f, ((y + across) % 2) * 2 * size + (along(x) % size) * 2 + c))
    return out


def on_device(query_rows, key_rows, value_rows, out_grad, out_weight, segment_ids):
    row_count, features = query_rows.shape
    fsdp_count = lax.axis_size("fsdp")
    rep_count = lax.axis_size("rep")
    size = fsdp_count // 4
    chips = fsdp_count // 2
    width = features // chips
    half, quarter = row_count // 2, row_count // 4
    me = lax.axis_index("fsdp")
    core, x, y = me % 2, (me // 2) % size, me // (2 * size)
    first = core == 0
    groups = [[2 * k + c for k in range(chips)] for c in range(2)]
    swap = [(f, f ^ 1) for f in range(fsdp_count)]

    def send(value, pairs, name):
        with jax.named_scope(name):
            return lax.ppermute(value, "fsdp", pairs)

    def mine(value, axis=0):
        low, high = jnp.split(value, 2, axis=axis)
        return jnp.where(first, low, high), jnp.where(first, high, low)

    right, left = moves(0, lambda i: i + 1, size), moves(0, lambda i: i - 1, size)
    over = moves(1, lambda i: i, size)

    near = out_grad[:half]
    near_left, near_right = send(near, right, "near_right"), send(near, left, "near_left")
    far = send(near, over, "far")
    far_left, far_right = send(far, right, "far_right"), send(far, left, "far_left")
    near_opposite = send(near_left, right, "near_opposite")
    far_opposite = send(far_right, left, "far_opposite")
    pieces = [near, far, near_left, near_right, far_left, far_right, near_opposite, far_opposite]
    places = [(0, 0), (1, 0), (0, -1), (0, 1), (1, -1), (1, 1), (0, 2), (1, 2)]
    order = jnp.stack(
        [((y + dy) % 2) * size + (x + dx + size) % size for dy, dx in places]
    ).astype(jnp.int32)

    weight_other = send(out_weight, swap, "weight")
    weight = jnp.concatenate(
        [jnp.where(first, out_weight, weight_other), jnp.where(first, weight_other, out_weight)]
    )

    extra = jnp.where((segment_ids[half:] >= 0)[:, None], out_grad[half:], 0)
    own, other = mine(extra)
    extra = own + send(other, swap, "extra_core")
    extra = extra + send(extra, over, "extra_over")
    extra = extra + send(extra, moves(0, lambda i: i ^ 1, size), "extra_even")
    extra = extra + send(extra, moves(0, lambda i: size - 1 - i, size), "extra_odd")

    attended, probs = attention_forward(query_rows, key_rows, value_rows, segment_ids)
    own, other = mine(attended[:, half:], axis=1)
    own = own + send(other, swap, "attended_core")
    with jax.named_scope("attended_out"):
        attended_in = lax.all_to_all(
            jnp.concatenate([attended[:, :half], own], axis=1),
            "fsdp",
            0,
            0,
            axis_index_groups=groups,
        )
    attended_extra = jnp.sum(attended_in[:, half:].astype(F32), axis=0).astype(BF16)

    extra_grad = dot(extra, weight, 1, 1).astype(BF16)
    to_send = jnp.zeros((chips, half + quarter, width), BF16)
    to_send = to_send.at[:, half:].set(jnp.broadcast_to(extra_grad, (chips,) + extra_grad.shape))
    for place, piece in enumerate(pieces):
        grad = dot(piece, weight, 1, 1).astype(BF16)
        to_send = lax.dynamic_update_slice(to_send, grad[None], (order[place], 0, 0))
    with jax.named_scope("grad_out"):
        grads = lax.all_to_all(to_send, "fsdp", 0, 0, axis_index_groups=groups)
    grads_other = send(grads[:, half:], swap, "grads_core")

    partial = weight_gradient(order, attended_in[:, :half], attended_extra, pieces, extra)
    own, other = mine(partial)
    group_part = (own + send(other.astype(BF16), swap, "weight_core").astype(F32)).astype(BF16)
    with jax.named_scope("rep_scatter"):
        parts = lax.all_to_all(group_part, "rep", 0, 0, tiled=True)
    parts = parts.reshape(rep_count, -1, features)
    total = jnp.sum(parts.astype(F32), axis=0).astype(BF16)
    with jax.named_scope("rep_gather"):
        total = lax.all_to_all(
            jnp.broadcast_to(total, (rep_count,) + total.shape), "rep", 0, 0
        )
    inverse_root = 1.0 / math.sqrt(row_count * fsdp_count * rep_count)
    weight_grad = total.reshape(-1, features).astype(F32) * inverse_root

    grad_query, grad_key, grad_value = attention_backward(
        core[None].astype(jnp.int32), query_rows, key_rows, value_rows, probs, attended, grads, grads_other
    )
    return grad_query, grad_key, grad_value, weight_grad


def solution(mesh):
    rows = P(("rep", "fsdp"), None)
    return jax.shard_map(
        on_device,
        mesh=mesh,
        in_specs=(rows, rows, rows, rows, P("fsdp", None), P(("rep", "fsdp"))),
        out_specs=(rows, rows, rows, P("fsdp", None)),
        check_vma=False,
    )
```

```python
import functools
import math

import jax
import jax.numpy as jnp
from jax import lax
from jax.experimental import pallas as pl
from jax.experimental.pallas import tpu as pltpu
from jax.sharding import PartitionSpec as P

E = 128
HEADS = 3
LOG2E = 1.4426950408889634
F32 = jnp.float32
BF16 = jnp.bfloat16


def dot(a, b, contract_a, contract_b):
    return lax.dot_general(
        a, b, (((contract_a,), (contract_b,)), ((), ())), preferred_element_type=F32
    )


def forward_kernel(q_ref, k_ref, v_ref, column_ref, row_ref, attended_ref, probs_ref):
    column, row = column_ref[...], row_ref[...]
    live = column >= 0
    bias = jnp.where((column == row) & live, 0.0, -1e30)
    for head in range(HEADS):
        at = slice(head * E, (head + 1) * E)
        logits = dot(q_ref[:, at], k_ref[:, at], 1, 1) * (LOG2E / math.sqrt(E)) + bias
        weights = jnp.exp2(logits - jnp.max(logits, axis=1, keepdims=True))
        total = jnp.sum(weights, axis=1, keepdims=True)
        probs = weights * jnp.where(live, 1.0 / total, 0.0)
        probs_ref[head] = probs
        attended_ref[0, :, at] = dot(probs.astype(BF16), v_ref[:, at], 1, 0).astype(BF16)


def attention_forward(query, key, value, segments):
    rows, features = query.shape
    width = HEADS * E
    steps = features // width
    whole = pl.BlockSpec((rows, width), lambda i: (0, i))
    return pl.pallas_call(
        forward_kernel,
        grid=(steps,),
        in_specs=[
            whole,
            whole,
            whole,
            pl.BlockSpec((rows, 1), lambda i: (0, 0)),
            pl.BlockSpec((1, rows), lambda i: (0, 0)),
        ],
        out_specs=[
            pl.BlockSpec((1, rows, width), lambda i: (i, 0, 0)),
            pl.BlockSpec((HEADS, rows, rows), lambda i: (i, 0, 0)),
        ],
        out_shape=[
            jax.ShapeDtypeStruct((steps, rows, width), BF16),
            jax.ShapeDtypeStruct((steps * HEADS, rows, rows), F32),
        ],
        cost_estimate=pl.CostEstimate(
            flops=8 * rows * rows * features,
            bytes_accessed=24 * rows * features,
            transcendentals=rows * rows * features // E,
        ),
        name="attention_forward",
    )(query, key, value, segments[:, None], segments[None, :])


def backward_kernel(
    core_ref, q_ref, k_ref, v_ref, probs_ref, attended_ref, ga_ref, own_ref, other_ref, dq_ref, dk_ref, dv_ref
):
    scale = 1.0 / math.sqrt(E)
    first = core_ref[0] == 0
    for head in range(HEADS):
        at = slice(head * E, (head + 1) * E)
        own, other = own_ref[0, :, at], other_ref[0, :, at]
        grad = jnp.concatenate(
            [ga_ref[0, :, at], jnp.where(first, own, other), jnp.where(first, other, own)], axis=0
        )
        probs = probs_ref[head]
        row_dot = jnp.sum(
            grad.astype(F32) * attended_ref[0, :, at].astype(F32), axis=1, keepdims=True
        )
        grad_logits = (probs * (dot(grad, v_ref[:, at], 1, 1) - row_dot)).astype(BF16)
        dq_ref[:, at] = (dot(grad_logits, k_ref[:, at], 1, 0) * scale).astype(BF16)
        dk_ref[:, at] = (dot(grad_logits, q_ref[:, at], 0, 0) * scale).astype(BF16)
        dv_ref[:, at] = dot(probs.astype(BF16), grad, 0, 0).astype(BF16)


def attention_backward(core, query, key, value, probs, attended, grads, own, other):
    rows, features = query.shape
    width = HEADS * E
    steps = features // width
    whole = pl.BlockSpec((rows, width), lambda i, c: (0, i))
    step = lambda a: pl.BlockSpec((1,) + a.shape[1:], lambda i, c: (i, 0, 0))
    return pl.pallas_call(
        backward_kernel,
        grid_spec=pltpu.PrefetchScalarGridSpec(
            num_scalar_prefetch=1,
            grid=(steps,),
            in_specs=[
                whole,
                whole,
                whole,
                pl.BlockSpec((HEADS, rows, rows), lambda i, c: (i, 0, 0)),
                step(attended),
                step(grads),
                step(own),
                step(other),
            ],
            out_specs=[whole, whole, whole],
        ),
        out_shape=[jax.ShapeDtypeStruct((rows, features), BF16)] * 3,
        cost_estimate=pl.CostEstimate(
            flops=16 * rows * rows * features,
            bytes_accessed=30 * rows * features,
            transcendentals=0,
        ),
        name="attention_backward",
    )(core, query, key, value, probs, attended, grads, own, other)


def weight_kernel(count, order_ref, att_ref, *refs):
    pieces, start_ref, out_ref = refs[:count], refs[count], refs[count + 1]
    total = start_ref[...]
    for place in range(count):
        total += dot(att_ref[order_ref[place]], pieces[place][...], 0, 0)
    out_ref[...] = total


def weight_extra_kernel(count, order_ref, att_ref, *refs):
    pieces, extra_ref, rows_ref, start_ref, out_ref = refs[:count], *refs[count:]
    total = start_ref[...] + dot(extra_ref[...], rows_ref[...], 0, 0)
    for place in range(count):
        total += dot(att_ref[order_ref[place]], pieces[place][...], 0, 0)
    out_ref[...] = total


def weight_first_kernel(count, order_ref, att_ref, *refs):
    pieces, out_ref = refs[:count], refs[count]
    total = dot(att_ref[order_ref[0]], pieces[0][...], 0, 0)
    for place in range(1, count):
        total += dot(att_ref[order_ref[place]], pieces[place][...], 0, 0)
    out_ref[...] = total


def weight_gradient(order, attended, pieces, extra=(), start=None, tile=512):
    count = len(pieces)
    rows, width = attended.shape[1:]
    features = pieces[0].shape[1]
    columns = lambda r: pl.BlockSpec((r, tile), lambda i, o: (0, i))
    in_specs = [pl.BlockSpec(attended.shape, lambda i, o: (0, 0, 0))] + [columns(rows)] * count
    operands = [attended, *pieces]
    kernel = weight_first_kernel
    if start is not None:
        kernel = weight_kernel
        if extra:
            kernel = weight_extra_kernel
            in_specs += [pl.BlockSpec(extra[0].shape, lambda i, o: (0, 0)), columns(extra[1].shape[0])]
            operands += list(extra)
        in_specs.append(columns(width))
        operands.append(start)
    return pl.pallas_call(
        functools.partial(kernel, count),
        grid_spec=pltpu.PrefetchScalarGridSpec(
            num_scalar_prefetch=1,
            grid=(features // tile,),
            in_specs=in_specs,
            out_specs=columns(width),
        ),
        out_shape=jax.ShapeDtypeStruct((width, features), F32),
        cost_estimate=pl.CostEstimate(
            flops=2 * width * features * count * rows,
            bytes_accessed=2 * features * (count * rows + 2 * width),
            transcendentals=0,
        ),
    )(order, *operands)


def moves(across, along, size):
    out = []
    for f in range(2 * 2 * size):
        y, x, c = f // (2 * size), (f // 2) % size, f % 2
        out.append((f, ((y + across) % 2) * 2 * size + (along(x) % size) * 2 + c))
    return out


def compute(query_rows, key_rows, value_rows, out_grad, out_weight, segment_ids):
    row_count, features = query_rows.shape
    fsdp_count = lax.axis_size("fsdp")
    rep_count = lax.axis_size("rep")
    size = fsdp_count // 4
    chips = fsdp_count // 2
    width = features // chips
    half = row_count // 2
    me = lax.axis_index("fsdp")
    core, x, y = me % 2, (me // 2) % size, me // (2 * size)
    first = core == 0
    groups = [[2 * k + c for k in range(chips)] for c in range(2)]
    swap = [(f, f ^ 1) for f in range(fsdp_count)]

    def send(value, pairs):
        return lax.ppermute(value, "fsdp", pairs)

    def mine(value, axis=0):
        low, high = jnp.split(value, 2, axis=axis)
        return jnp.where(first, low, high), jnp.where(first, high, low)

    right, left = moves(0, lambda i: i + 1, size), moves(0, lambda i: i - 1, size)
    over = moves(1, lambda i: i, size)

    near = out_grad[:half]
    near_left, near_right = send(near, right), send(near, left)
    far = send(near, over)
    far_left, far_right = send(far, right), send(far, left)
    near_opposite = send(near_left, right)
    far_opposite = send(far_right, left)
    pieces = [near, far, near_left, near_right, far_left, far_right, near_opposite, far_opposite]
    places = [(0, 0), (1, 0), (0, -1), (0, 1), (1, -1), (1, 1), (0, 2), (1, 2)]
    order = jnp.stack(
        [((y + dy) % 2) * size + (x + dx + size) % size for dy, dx in places]
    ).astype(jnp.int32)

    weight_other = send(out_weight, swap)
    weight = jnp.concatenate(
        [jnp.where(first, out_weight, weight_other), jnp.where(first, weight_other, out_weight)]
    )

    extra = jnp.where((segment_ids[half:] >= 0)[:, None], out_grad[half:], 0)
    own, other = mine(extra)
    extra = own + send(other, swap)
    extra = extra + send(extra, over)
    extra = extra + send(extra, moves(0, lambda i: i ^ 1, size))
    extra = extra + send(extra, moves(0, lambda i: size - 1 - i, size))

    attended, probs = attention_forward(query_rows, key_rows, value_rows, segment_ids)
    own, other = mine(attended[:, half:], axis=1)
    own = own + send(other, swap)
    attended_in = lax.all_to_all(
        jnp.concatenate([attended[:, :half], own], axis=1),
        "fsdp",
        0,
        0,
        axis_index_groups=groups,
    )
    attended_extra = jnp.sum(attended_in[:, half:].astype(F32), axis=0).astype(BF16)
    attended_in = attended_in[:, :half]

    to_send = jnp.zeros((chips, half, width), BF16)
    for place, piece in enumerate(pieces):
        grad = dot(piece, weight, 1, 1).astype(BF16)
        to_send = lax.dynamic_update_slice(to_send, grad[None], (order[place], 0, 0))
    grads = lax.all_to_all(to_send, "fsdp", 0, 0, axis_index_groups=groups)

    extra_grad = dot(extra, weight, 1, 1).astype(BF16)
    extra_grad = jnp.broadcast_to(extra_grad, (chips,) + extra_grad.shape)
    grads_own = lax.all_to_all(extra_grad, "fsdp", 0, 0, axis_index_groups=groups)
    grads_other = send(grads_own, swap)

    early = len(pieces) - 2
    partial = weight_gradient(order, attended_in, pieces[:early])
    partial = weight_gradient(
        order[early:], attended_in, pieces[early:], (attended_extra, extra), partial
    )
    own, other = mine(partial)
    group_part = (own + send(other.astype(BF16), swap).astype(F32)).astype(BF16)
    weight_grad = sum_over_groups(group_part, 1.0 / math.sqrt(row_count * fsdp_count * rep_count))

    grad_query, grad_key, grad_value = attention_backward(
        core[None].astype(jnp.int32),
        query_rows,
        key_rows,
        value_rows,
        probs,
        attended,
        grads,
        grads_own,
        grads_other,
    )
    return grad_query, grad_key, grad_value, weight_grad


def sum_over_groups(part, scale):
    count = lax.axis_size("rep")
    depth = count // 2
    rows = part.shape[0] // count
    me = lax.axis_index("rep")
    shifts = [(dy, dz) for dy in range(2) for dz in range(depth)][1:]

    def peer(index, shift):
        return (index // depth + shift[0]) % 2 * depth + (index % depth + shift[1]) % depth

    def cut(index):
        return lax.dynamic_slice(part, (index * rows, 0), (rows, part.shape[1]))

    total = cut(me).astype(F32)
    for shift in shifts:
        pairs = [(r, peer(r, shift)) for r in range(count)]
        total = total + lax.ppermute(cut(peer(me, shift)), "rep", pairs).astype(F32)
    total = total.astype(BF16)
    out = jnp.zeros((count, rows, part.shape[1]), F32)
    out = lax.dynamic_update_slice(out, (total.astype(F32) * scale)[None], (me, 0, 0))
    for shift in shifts:
        pairs = [(peer(r, shift), r) for r in range(count)]
        other = lax.ppermute(total, "rep", pairs)
        out = lax.dynamic_update_slice(
            out, (other.astype(F32) * scale)[None], (peer(me, shift), 0, 0)
        )
    return out.reshape(part.shape)


def solution(mesh):
    rows = P(("rep", "fsdp"), None)
    return jax.shard_map(
        compute,
        mesh=mesh,
        in_specs=(rows, rows, rows, rows, P("fsdp", None), P(("rep", "fsdp"))),
        out_specs=(rows, rows, rows, P("fsdp", None)),
        check_vma=False,
    )
```

```python
import functools
import math

import jax
import jax.numpy as jnp
from jax import lax
from jax.experimental import pallas as pl
from jax.experimental.pallas import tpu as pltpu
from jax.sharding import PartitionSpec as P

E = 128
HEADS = 3
LOG2E = 1.4426950408889634
F32 = jnp.float32
BF16 = jnp.bfloat16


def dot(a, b, contract_a, contract_b):
    return lax.dot_general(
        a, b, (((contract_a,), (contract_b,)), ((), ())), preferred_element_type=F32
    )


def forward_kernel(q_ref, k_ref, v_ref, column_ref, row_ref, attended_ref, probs_ref):
    column, row = column_ref[...], row_ref[...]
    live = column >= 0
    bias = jnp.where((column == row) & live, 0.0, -1e30)
    for head in range(HEADS):
        at = slice(head * E, (head + 1) * E)
        logits = dot(q_ref[:, at], k_ref[:, at], 1, 1) * (LOG2E / math.sqrt(E)) + bias
        weights = jnp.exp2(logits - jnp.max(logits, axis=1, keepdims=True))
        total = jnp.sum(weights, axis=1, keepdims=True)
        probs = weights * jnp.where(live, 1.0 / total, 0.0)
        probs_ref[head] = probs
        attended_ref[0, :, at] = dot(probs.astype(BF16), v_ref[:, at], 1, 0).astype(BF16)


def attention_forward(query, key, value, segments):
    rows, features = query.shape
    width = HEADS * E
    steps = features // width
    whole = pl.BlockSpec((rows, width), lambda i: (0, i))
    return pl.pallas_call(
        forward_kernel,
        grid=(steps,),
        in_specs=[
            whole,
            whole,
            whole,
            pl.BlockSpec((rows, 1), lambda i: (0, 0)),
            pl.BlockSpec((1, rows), lambda i: (0, 0)),
        ],
        out_specs=[
            pl.BlockSpec((1, rows, width), lambda i: (i, 0, 0)),
            pl.BlockSpec((HEADS, rows, rows), lambda i: (i, 0, 0)),
        ],
        out_shape=[
            jax.ShapeDtypeStruct((steps, rows, width), BF16),
            jax.ShapeDtypeStruct((steps * HEADS, rows, rows), F32),
        ],
        cost_estimate=pl.CostEstimate(
            flops=8 * rows * rows * features,
            bytes_accessed=24 * rows * features,
            transcendentals=rows * rows * features // E,
        ),
        name="attention_forward",
    )(query, key, value, segments[:, None], segments[None, :])


def backward_kernel(count, order_ref, q_ref, k_ref, v_ref, probs_ref, attended_ref, own_ref, other_ref, *refs):
    blocks, (dq_ref, dk_ref, dv_ref, grad_ref) = refs[:count], refs[count:]
    scale = 1.0 / math.sqrt(E)
    half, quarter = blocks[0].shape[0], own_ref.shape[1]
    for place in range(count):

        @pl.when(pl.program_id(0) == place)
        def _(place=place):
            grad_ref[:half] = blocks[place][...]

    first = order_ref[count] == 0
    own, other = own_ref[0], other_ref[0]
    grad_ref[half : half + quarter] = jnp.where(first, own, other)
    grad_ref[half + quarter :] = jnp.where(first, other, own)
    for head in range(HEADS):
        at = slice(head * E, (head + 1) * E)
        grad = grad_ref[:, at]
        probs = probs_ref[head]
        row_dot = jnp.sum(
            grad.astype(F32) * attended_ref[0, :, at].astype(F32), axis=1, keepdims=True
        )
        grad_logits = (probs * (dot(grad, v_ref[:, at], 1, 1) - row_dot)).astype(BF16)
        dq_ref[:, at] = (dot(grad_logits, k_ref[:, at], 1, 0) * scale).astype(BF16)
        dk_ref[:, at] = (dot(grad_logits, q_ref[:, at], 0, 0) * scale).astype(BF16)
        dv_ref[:, at] = dot(probs.astype(BF16), grad, 0, 0).astype(BF16)


def attention_backward(order, query, key, value, probs, attended, own, other, blocks):
    rows, features = query.shape
    width = HEADS * E
    steps = features // width
    whole = pl.BlockSpec((rows, width), lambda i, o: (0, o[i]))
    step = lambda a: pl.BlockSpec((1,) + a.shape[1:], lambda i, o: (o[i], 0, 0))
    return pl.pallas_call(
        functools.partial(backward_kernel, steps),
        grid_spec=pltpu.PrefetchScalarGridSpec(
            num_scalar_prefetch=1,
            grid=(steps,),
            in_specs=[
                whole,
                whole,
                whole,
                pl.BlockSpec((HEADS, rows, rows), lambda i, o: (o[i], 0, 0)),
                step(attended),
                step(own),
                step(other),
            ]
            + [pl.BlockSpec(blocks[0].shape, lambda i, o: (0, 0))] * steps,
            out_specs=[whole, whole, whole],
            scratch_shapes=[pltpu.VMEM((rows, width), BF16)],
        ),
        out_shape=[jax.ShapeDtypeStruct((rows, features), BF16)] * 3,
        cost_estimate=pl.CostEstimate(
            flops=16 * rows * rows * features,
            bytes_accessed=30 * rows * features,
            transcendentals=0,
        ),
        name="attention_backward",
    )(order, query, key, value, probs, attended, own, other, *blocks)


def weight_first_kernel(count, order_ref, att_ref, *refs):
    pieces, out_ref = refs[:count], refs[count]
    total = dot(att_ref[order_ref[0]], pieces[0][...], 1, 0)
    for place in range(1, count):
        total += dot(att_ref[order_ref[place]], pieces[place][...], 1, 0)
    out_ref[...] = total


def weight_last_kernel(count, order_ref, att_ref, *refs):
    pieces = refs[:count]
    extra_ref, rows_ref, start_ref, own_ref, other_ref = refs[count:]
    total = start_ref[...] + dot(extra_ref[...], rows_ref[...], 1, 0)
    for place in range(count):
        total += dot(att_ref[order_ref[place]], pieces[place][...], 1, 0)
    half = own_ref.shape[0]
    first = order_ref[count] == 0
    own_ref[...] = jnp.where(first, total[:half], total[half:])
    other_ref[...] = jnp.where(first, total[half:], total[:half]).astype(other_ref.dtype)


def weight_gradient(order, attended, pieces, extra=None, start=None, tile=512):
    count = len(pieces)
    width, rows = attended.shape[1:]
    features = pieces[0].shape[1]
    columns = lambda r: pl.BlockSpec((r, tile), lambda i, o: (0, i))
    in_specs = [pl.BlockSpec(attended.shape, lambda i, o: (0, 0, 0))] + [columns(rows)] * count
    operands = [attended, *pieces]
    if start is None:
        kernel = weight_first_kernel
        out_specs = columns(width)
        out_shape = jax.ShapeDtypeStruct((width, features), F32)
    else:
        kernel = weight_last_kernel
        in_specs += [
            pl.BlockSpec(extra[0].shape, lambda i, o: (0, 0)),
            columns(extra[1].shape[0]),
            columns(width),
        ]
        operands += [*extra, start]
        out_specs = [columns(width // 2)] * 2
        out_shape = [jax.ShapeDtypeStruct((width // 2, features), d) for d in (F32, BF16)]
    return pl.pallas_call(
        functools.partial(kernel, count),
        grid_spec=pltpu.PrefetchScalarGridSpec(
            num_scalar_prefetch=1, grid=(features // tile,), in_specs=in_specs, out_specs=out_specs
        ),
        out_shape=out_shape,
        cost_estimate=pl.CostEstimate(
            flops=2 * width * features * count * rows,
            bytes_accessed=2 * features * (count * rows + 2 * width),
            transcendentals=0,
        ),
    )(order, *operands)


def moves(across, along, size):
    out = []
    for f in range(2 * 2 * size):
        y, x, c = f // (2 * size), (f // 2) % size, f % 2
        out.append((f, ((y + across) % 2) * 2 * size + (along(x) % size) * 2 + c))
    return out


def compute(query_rows, key_rows, value_rows, out_grad, out_weight, segment_ids):
    row_count, features = query_rows.shape
    fsdp_count = lax.axis_size("fsdp")
    rep_count = lax.axis_size("rep")
    size = fsdp_count // 4
    chips = fsdp_count // 2
    half = row_count // 2
    me = lax.axis_index("fsdp")
    core, x, y = me % 2, (me // 2) % size, me // (2 * size)
    first = core == 0
    groups = [[2 * k + c for k in range(chips)] for c in range(2)]
    swap = [(f, f ^ 1) for f in range(fsdp_count)]

    def send(value, pairs):
        return lax.ppermute(value, "fsdp", pairs)

    def mine(value, axis=0):
        low, high = jnp.split(value, 2, axis=axis)
        return jnp.where(first, low, high), jnp.where(first, high, low)

    right, left = moves(0, lambda i: i + 1, size), moves(0, lambda i: i - 1, size)
    over = moves(1, lambda i: i, size)

    near = out_grad[:half]
    near_left, near_right = send(near, right), send(near, left)
    far = send(near, over)
    far_left, far_right = send(far, right), send(far, left)
    near_opposite = send(near_left, right)
    far_opposite = send(far_right, left)
    pieces = [near, far, near_left, near_right, far_left, far_right, near_opposite, far_opposite]
    places = [(0, 0), (1, 0), (0, -1), (0, 1), (1, -1), (1, 1), (0, 2), (1, 2)]
    turns = jnp.array(places, jnp.int32)
    order = (y + turns[:, 0]) % 2 * size + (x + turns[:, 1] + size) % size
    owners = (y + turns[:, 0]) % 2 * size + (x - turns[:, 1] + size) % size
    order = order.astype(jnp.int32)
    owners = jnp.append(owners, core).astype(jnp.int32)

    weight_other = send(out_weight, swap)
    weight = jnp.concatenate(
        [jnp.where(first, out_weight, weight_other), jnp.where(first, weight_other, out_weight)]
    )

    extra = jnp.where((segment_ids[half:] >= 0)[:, None], out_grad[half:], 0)
    own, other = mine(extra)
    extra = own + send(other, swap)
    extra = extra + send(extra, over)
    extra = extra + send(extra, moves(0, lambda i: i ^ 1, size))
    extra = extra + send(extra, moves(0, lambda i: size - 1 - i, size))

    attended, probs = attention_forward(query_rows, key_rows, value_rows, segment_ids)
    own, other = mine(attended[:, half:], axis=1)
    own = own + send(other, swap)
    attended_in = lax.all_to_all(
        jnp.concatenate([attended[:, :half], own], axis=1),
        "fsdp",
        0,
        0,
        axis_index_groups=groups,
    )
    attended_extra = jnp.sum(attended_in[:, half:].astype(F32), axis=0).astype(BF16).T
    attended_in = jnp.swapaxes(attended_in[:, :half], 1, 2)

    blocks = []
    for n, (piece, (dy, dx)) in enumerate(zip(pieces, places)):
        grad = dot(piece, weight, 1, 1).astype(BF16)
        if n:
            grad = send(grad, moves(dy, lambda i: i + dx + size, size))
        blocks.append(grad)

    extra_grad = dot(extra, weight, 1, 1).astype(BF16)
    extra_grad = jnp.broadcast_to(extra_grad, (chips,) + extra_grad.shape)
    grads_own = lax.all_to_all(extra_grad, "fsdp", 0, 0, axis_index_groups=groups)
    grads_other = send(grads_own, swap)

    early = len(pieces) - 2
    partial = weight_gradient(order, attended_in, pieces[:early])
    own, other = weight_gradient(
        jnp.append(order[early:], core.astype(jnp.int32)),
        attended_in,
        pieces[early:],
        (attended_extra, extra),
        partial,
    )
    group_part = (own + send(other, swap).astype(F32)).astype(BF16)
    parts = lax.all_to_all(group_part, "rep", 0, 0, tiled=True)
    parts = parts.reshape(rep_count, -1, features)
    total = jnp.sum(parts.astype(F32), axis=0).astype(BF16)
    total = lax.all_to_all(
        jnp.broadcast_to(total, (rep_count,) + total.shape), "rep", 0, 0
    )
    inverse_root = 1.0 / math.sqrt(row_count * fsdp_count * rep_count)
    weight_grad = total.reshape(-1, features).astype(F32) * inverse_root

    grad_query, grad_key, grad_value = attention_backward(
        owners,
        query_rows,
        key_rows,
        value_rows,
        probs,
        attended,
        grads_own,
        grads_other,
        blocks,
    )
    return grad_query, grad_key, grad_value, weight_grad


def solution(mesh):
    rows = P(("rep", "fsdp"), None)
    return jax.shard_map(
        compute,
        mesh=mesh,
        in_specs=(rows, rows, rows, rows, P("fsdp", None), P(("rep", "fsdp"))),
        out_specs=(rows, rows, rows, P("fsdp", None)),
        check_vma=False,
    )
```

```python
import functools
import math

import jax
import jax.numpy as jnp
from jax import lax
from jax.experimental import pallas as pl
from jax.experimental.pallas import tpu as pltpu
from jax.sharding import PartitionSpec as P

E = 128
HEADS = 3
LOG2E = 1.4426950408889634
F32 = jnp.float32
BF16 = jnp.bfloat16


def dot(a, b, contract_a, contract_b):
    return lax.dot_general(
        a, b, (((contract_a,), (contract_b,)), ((), ())), preferred_element_type=F32
    )


def forward_kernel(q_ref, k_ref, v_ref, column_ref, row_ref, attended_ref, probs_ref):
    column, row = column_ref[...], row_ref[...]
    live = column >= 0
    bias = jnp.where((column == row) & live, 0.0, -1e30)
    for head in range(HEADS):
        at = slice(head * E, (head + 1) * E)
        logits = dot(q_ref[:, at], k_ref[:, at], 1, 1) * (LOG2E / math.sqrt(E)) + bias
        weights = jnp.exp2(logits - jnp.max(logits, axis=1, keepdims=True))
        total = jnp.sum(weights, axis=1, keepdims=True)
        probs = weights * jnp.where(live, 1.0 / total, 0.0)
        probs_ref[head] = probs
        attended_ref[0, :, at] = dot(probs.astype(BF16), v_ref[:, at], 1, 0).astype(BF16)


def attention_forward(query, key, value, segments):
    rows, features = query.shape
    width = HEADS * E
    steps = features // width
    whole = pl.BlockSpec((rows, width), lambda i: (0, i))
    return pl.pallas_call(
        forward_kernel,
        grid=(steps,),
        in_specs=[
            whole,
            whole,
            whole,
            pl.BlockSpec((rows, 1), lambda i: (0, 0)),
            pl.BlockSpec((1, rows), lambda i: (0, 0)),
        ],
        out_specs=[
            pl.BlockSpec((1, rows, width), lambda i: (i, 0, 0)),
            pl.BlockSpec((HEADS, rows, rows), lambda i: (i, 0, 0)),
        ],
        out_shape=[
            jax.ShapeDtypeStruct((steps, rows, width), BF16),
            jax.ShapeDtypeStruct((steps * HEADS, rows, rows), F32),
        ],
        cost_estimate=pl.CostEstimate(
            flops=8 * rows * rows * features,
            bytes_accessed=24 * rows * features,
            transcendentals=rows * rows * features // E,
        ),
        name="attention_forward",
    )(query, key, value, segments[:, None], segments[None, :])


def backward_kernel(
    core_ref, q_ref, k_ref, v_ref, probs_ref, attended_ref, ga_ref, other_ref, dq_ref, dk_ref, dv_ref
):
    scale = 1.0 / math.sqrt(E)
    half = ga_ref.shape[1] - other_ref.shape[1]
    first = core_ref[0] == 0
    for head in range(HEADS):
        at = slice(head * E, (head + 1) * E)
        own, other = ga_ref[0, half:, at], other_ref[0, :, at]
        grad = jnp.concatenate(
            [ga_ref[0, :half, at], jnp.where(first, own, other), jnp.where(first, other, own)], axis=0
        )
        probs = probs_ref[head]
        row_dot = jnp.sum(
            grad.astype(F32) * attended_ref[0, :, at].astype(F32), axis=1, keepdims=True
        )
        grad_logits = (probs * (dot(grad, v_ref[:, at], 1, 1) - row_dot)).astype(BF16)
        dq_ref[:, at] = (dot(grad_logits, k_ref[:, at], 1, 0) * scale).astype(BF16)
        dk_ref[:, at] = (dot(grad_logits, q_ref[:, at], 0, 0) * scale).astype(BF16)
        dv_ref[:, at] = dot(probs.astype(BF16), grad, 0, 0).astype(BF16)


def attention_backward(core, query, key, value, probs, attended, grads, other):
    rows, features = query.shape
    width = HEADS * E
    steps = features // width
    whole = pl.BlockSpec((rows, width), lambda i, c: (0, i))
    step = lambda a: pl.BlockSpec((1,) + a.shape[1:], lambda i, c: (i, 0, 0))
    return pl.pallas_call(
        backward_kernel,
        grid_spec=pltpu.PrefetchScalarGridSpec(
            num_scalar_prefetch=1,
            grid=(steps,),
            in_specs=[
                whole,
                whole,
                whole,
                pl.BlockSpec((HEADS, rows, rows), lambda i, c: (i, 0, 0)),
                step(attended),
                step(grads),
                step(other),
            ],
            out_specs=[whole, whole, whole],
        ),
        out_shape=[jax.ShapeDtypeStruct((rows, features), BF16)] * 3,
        cost_estimate=pl.CostEstimate(
            flops=16 * rows * rows * features,
            bytes_accessed=30 * rows * features,
            transcendentals=0,
        ),
        name="attention_backward",
    )(core, query, key, value, probs, attended, grads, other)


def weight_kernel(count, order_ref, att_ref, *refs):
    pieces = refs[:count]
    extra_ref, rows_ref, own_ref, other_ref = refs[count:]
    total = dot(extra_ref[...], rows_ref[...], 1, 0)
    for place in range(count):
        total += dot(att_ref[order_ref[place]], pieces[place][...], 1, 0)
    half = own_ref.shape[0]
    first = order_ref[count] == 0
    own_ref[...] = jnp.where(first, total[:half], total[half:])
    other_ref[...] = jnp.where(first, total[half:], total[:half]).astype(other_ref.dtype)


def weight_gradient(order, attended, pieces, attended_extra, extra, tile=512):
    count = len(pieces)
    width, rows = attended.shape[1:]
    features = pieces[0].shape[1]
    columns = lambda r: pl.BlockSpec((r, tile), lambda i, o: (0, i))
    return pl.pallas_call(
        functools.partial(weight_kernel, count),
        grid_spec=pltpu.PrefetchScalarGridSpec(
            num_scalar_prefetch=1,
            grid=(features // tile,),
            in_specs=[pl.BlockSpec(attended.shape, lambda i, o: (0, 0, 0))]
            + [columns(rows)] * count
            + [pl.BlockSpec(attended_extra.shape, lambda i, o: (0, 0)), columns(extra.shape[0])],
            out_specs=[columns(width // 2)] * 2,
        ),
        out_shape=[jax.ShapeDtypeStruct((width // 2, features), d) for d in (F32, BF16)],
        cost_estimate=pl.CostEstimate(
            flops=2 * width * features * count * rows,
            bytes_accessed=2 * features * (count * rows + 2 * width),
            transcendentals=0,
        ),
        name="weight_gradient",
    )(order, attended, *pieces, attended_extra, extra)


def moves(across, along, size):
    out = []
    for f in range(2 * 2 * size):
        y, x, c = f // (2 * size), (f // 2) % size, f % 2
        out.append((f, ((y + across) % 2) * 2 * size + (along(x) % size) * 2 + c))
    return out


def compute(query_rows, key_rows, value_rows, out_grad, out_weight, segment_ids):
    row_count, features = query_rows.shape
    fsdp_count = lax.axis_size("fsdp")
    rep_count = lax.axis_size("rep")
    size = fsdp_count // 4
    chips = fsdp_count // 2
    width = features // chips
    half, quarter = row_count // 2, row_count // 4
    me = lax.axis_index("fsdp")
    core, x, y = me % 2, (me // 2) % size, me // (2 * size)
    first = core == 0
    groups = [[2 * k + c for k in range(chips)] for c in range(2)]
    swap = [(f, f ^ 1) for f in range(fsdp_count)]

    def send(value, pairs):
        return lax.ppermute(value, "fsdp", pairs)

    def mine(value, axis=0):
        low, high = jnp.split(value, 2, axis=axis)
        return jnp.where(first, low, high), jnp.where(first, high, low)

    right, left = moves(0, lambda i: i + 1, size), moves(0, lambda i: i - 1, size)
    over = moves(1, lambda i: i, size)

    near = out_grad[:half]
    near_left, near_right = send(near, right), send(near, left)
    far = send(near, over)
    far_left_top = send(far[:quarter], right)
    far_right_bottom = send(far[quarter:], left)
    far_left_bottom = send(near_left[quarter:], over)
    far_right_top = send(near_right[:quarter], over)
    near_top = send(near_left[:quarter], right)
    near_bottom = send(near_right[quarter:], left)
    far_top = send(far_left_top, right)
    far_bottom = send(far_right_bottom, left)
    far_left = jnp.concatenate([far_left_top, far_left_bottom])
    far_right = jnp.concatenate([far_right_top, far_right_bottom])
    near_opposite = jnp.concatenate([near_top, near_bottom])
    far_opposite = jnp.concatenate([far_top, far_bottom])
    pieces = [near, far, near_left, near_right, far_left, far_right, near_opposite, far_opposite]
    places = [(0, 0), (1, 0), (0, -1), (0, 1), (1, -1), (1, 1), (0, 2), (1, 2)]
    turns = jnp.array(places, jnp.int32)
    order = (y + turns[:, 0]) % 2 * size + (x + turns[:, 1] + size) % size
    order = jnp.append(order, core).astype(jnp.int32)

    weight_other = send(out_weight, swap)
    weight = jnp.concatenate(
        [jnp.where(first, out_weight, weight_other), jnp.where(first, weight_other, out_weight)]
    )

    extra = jnp.where((segment_ids[half:] >= 0)[:, None], out_grad[half:], 0)
    own, other = mine(extra)
    extra = own + send(other, swap)
    low, high = jnp.split(extra, 2)
    extra = jnp.where(y == 0, low, high) + send(jnp.where(y == 0, high, low), over)
    extra = extra + send(extra, moves(0, lambda i: i ^ 1, size))
    extra = extra + send(extra, moves(0, lambda i: size - 1 - i, size))
    other = send(extra, over)
    extra = jnp.concatenate([jnp.where(y == 0, extra, other), jnp.where(y == 0, other, extra)])

    attended, probs = attention_forward(query_rows, key_rows, value_rows, segment_ids)
    own, other = mine(attended[:, half:], axis=1)
    own = own + send(other, swap)
    attended_in = lax.all_to_all(
        jnp.concatenate([attended[:, :half], own], axis=1),
        "fsdp",
        0,
        0,
        axis_index_groups=groups,
    )
    attended_extra = jnp.sum(attended_in[:, half:].astype(F32), axis=0).astype(BF16).T
    attended_in = jnp.swapaxes(attended_in[:, :half], 1, 2)

    to_send = jnp.zeros((chips, half + quarter, width), BF16)
    for n, piece in enumerate(pieces):
        grad = dot(piece, weight, 1, 1).astype(BF16)
        to_send = lax.dynamic_update_slice(to_send, grad[None], (order[n], 0, 0))
    extra_grad = dot(extra, weight, 1, 1).astype(BF16)
    to_send = to_send.at[:, half:].set(jnp.broadcast_to(extra_grad, (chips,) + extra_grad.shape))
    grads = lax.all_to_all(to_send, "fsdp", 0, 0, axis_index_groups=groups)
    grads_other = send(grads[:, half:], swap)

    own, other = weight_gradient(order, attended_in, pieces, attended_extra, extra)
    group_part = (own + send(other, swap).astype(F32)).astype(BF16)
    parts = lax.all_to_all(group_part, "rep", 0, 0, tiled=True)
    parts = parts.reshape(rep_count, -1, features)
    total = jnp.sum(parts.astype(F32), axis=0).astype(BF16)
    total = lax.all_to_all(
        jnp.broadcast_to(total, (rep_count,) + total.shape), "rep", 0, 0
    )
    inverse_root = 1.0 / math.sqrt(row_count * fsdp_count * rep_count)
    weight_grad = total.reshape(-1, features).astype(F32) * inverse_root

    grad_query, grad_key, grad_value = attention_backward(
        core[None].astype(jnp.int32), query_rows, key_rows, value_rows, probs, attended, grads, grads_other
    )
    return grad_query, grad_key, grad_value, weight_grad


def solution(mesh):
    rows = P(("rep", "fsdp"), None)
    return jax.shard_map(
        compute,
        mesh=mesh,
        in_specs=(rows, rows, rows, rows, P("fsdp", None), P(("rep", "fsdp"))),
        out_specs=(rows, rows, rows, P("fsdp", None)),
        check_vma=False,
    )
```
